32 devices in a mesh: groups: 2 (over y), seq: 8 (over z, core), dp: 2 (over x).
Axes of the slice: x: 2, y: 2, z: 4, core: 2. Of those that a mesh axis runs over, the one named last changes fastest.
Arguments:
- tokens: bfloat16 [4, 1024, 1024], P(('groups', 'dp'), 'seq'), parts along dimension 0, may hold values from -6 to 6
- w_query: bfloat16 [1024, 1024], replicated, may hold values from -0.1875 to 0.1875
- w_key: bfloat16 [1024, 1024], replicated, may hold values from -0.1875 to 0.1875
- w_value: bfloat16 [1024, 1024], replicated, may hold values from -0.1875 to 0.1875
- w_output: bfloat16 [1024, 1024], replicated, may hold values from -0.1875 to 0.1875
- out_cotangent: bfloat16 [4, 1024, 1024], P(('groups', 'dp'), 'seq'), parts along dimension 0, may hold values from -6 to 6
Outputs:
- attended: bfloat16 [4, 1024, 1024], P(('groups', 'dp'), 'seq'), parts along dimension 0
- d_tokens: bfloat16 [4, 1024, 1024], P(('groups', 'dp'), 'seq'), parts along dimension 0
- weight_grads: float32 [2048, 4096], P(('groups', 'seq', 'dp')), parts along dimension 0
The draws below stay inside these ranges and needn't reach their ends.
There are 2 independent parts, one for each index of `groups`. The reference program is written for one: setup_inputs(seed, part) draws one part's arguments, and reference() takes and returns one part's arrays. A program takes and returns all parts, laid end to end along the dimension named above; an argument that names none is the same for every part. Nothing has to cross between parts.
All inputs are finite; a program needn't handle non-finite values.
Results may differ from the reference program's by a relative error of at most 0.008.
Values sent between devices are 32-bit elements; how exact they have to be, the bound alone decides.
No kernel may reach another device: no remote copies, remote signals or barrier semaphores. Data moves between devices by JAX's collectives and lax.ppermute only.
A program may use at most 128 MiB of HBM per device.

```python
import math
import jax
import jax.numpy as jnp
from jax import lax

D = 1024
H = 8
DH = 128
TOK_DEV = 128
CLIPS = 2
LENGTH = 1024
N_SEQ = 8


def spiked(values, stream_key, source, target, parts, factor):
    owner, partner = [(jnp.arange(values.shape[axis_at]) // (values.shape[axis_at] // parts)).reshape([-1 if axis == axis_at else 1 for axis in range(values.ndim)]) for axis_at in (source, target)]
    chosen = jax.random.permutation(stream_key, parts)[partner]
    strong = (owner == chosen) | (owner == (partner + parts // 2) % parts)
    return jnp.where(strong, factor * values, values)


def levels(key, shape, shards, least, high):
    def one(dim, parts):
        draws = jax.random.uniform(jax.random.fold_in(jax.random.fold_in(key, 6), dim), (parts,), jnp.float32, least / len(shards), high / len(shards))
        return jnp.repeat(jnp.exp(draws), shape[dim] // parts).reshape((-1,) + (1,) * (len(shape) - dim - 1))

    gain = one(*shards[0])
    for cut in shards[1:]:
        gain = gain * one(*cut)
    return gain


def noise(own_key, dims, spread, most, split=(), dtype=jnp.bfloat16):
    values = jax.random.normal(own_key, dims, jnp.float32) * spread
    if len(split) > 0:
        values = levels(own_key, dims, split, -0.22, 0.18) * values
    return jnp.clip(values, min=-most, max=most).astype(dtype)


def heavy_noise(rng, shape, scale, bound, cuts, heavy, held_as=jnp.bfloat16):
    values = scale * jax.random.normal(rng, shape, jnp.float32)
    if cuts:
        values = values * levels(rng, shape, cuts, -0.22, 0.18)
    return jnp.clip(spiked(values, jax.random.fold_in(rng, 3), *heavy), -bound, bound).astype(held_as)


def setup_inputs(seed: int = 0, part: int = 0) -> dict:
    splits = jax.random.split(jax.random.key(seed), 7)
    part_splits = jax.random.split(jax.random.fold_in(splits[6], part), 7)
    tokens = heavy_noise(part_splits[0], (CLIPS, LENGTH, D), 1.0, 6.0, ((0, 2), (1, 8)), (1, 2, 8, 2.0))
    w_query = noise(splits[1], (D, D), D ** -0.5, 0.1875)
    w_key = noise(splits[2], (D, D), D ** -0.5, 0.1875)
    w_value = noise(splits[3], (D, D), D ** -0.5, 0.1875)
    w_output = noise(splits[4], (D, D), D ** -0.5, 0.1875)
    out_cotangent = noise(part_splits[5], (CLIPS, LENGTH, D), 1.0, 6.0, ((0, 2), (1, 8)))
    return dict(tokens=tokens, w_query=w_query, w_key=w_key, w_value=w_value, w_output=w_output, out_cotangent=out_cotangent)


EPSILON = 1e-05

def to_blocks(array):
    clip_count = array.shape[0]
    return array.reshape(clip_count, N_SEQ, TOK_DEV, H, DH).transpose(1, 0, 2, 3, 4)

def from_blocks(array):
    clip_count = array.shape[1]
    return array.transpose(1, 0, 2, 3, 4).reshape(clip_count, N_SEQ * TOK_DEV, H * DH)

def causal_mask(row_count):
    rows = lax.broadcasted_iota(jnp.int32, (row_count, row_count), 0)
    cols = lax.broadcasted_iota(jnp.int32, (row_count, row_count), 1)
    return rows >= cols

def project(flattened, weight):
    return jnp.dot(flattened, weight, preferred_element_type=jnp.float32).astype(jnp.bfloat16)

def forward_block(operands):
    queries, key_rows, value_rows, carried = operands
    causal = causal_mask(queries.shape[1])
    scores = jnp.einsum('cthd,cshd->chts', queries.astype(jnp.float32), key_rows.astype(jnp.float32))
    attn_weights = jnp.where(causal, scores, 0.0).astype(jnp.bfloat16)
    local_part = jnp.einsum('chts,cshd->cthd', attn_weights.astype(jnp.float32), value_rows.astype(jnp.float32))
    carried_part = jnp.einsum('cthd,chde->cthe', queries.astype(jnp.float32), carried.astype(jnp.float32))
    return local_part + carried_part

def backward_block(operands):
    queries, key_rows, value_rows, carried, later, d_heads = operands
    causal = causal_mask(queries.shape[1])
    qf = queries.astype(jnp.float32)
    kf = key_rows.astype(jnp.float32)
    vf = value_rows.astype(jnp.float32)
    gf = d_heads.astype(jnp.float32)
    cf = carried.astype(jnp.float32)
    lf = later.astype(jnp.float32)
    scores = jnp.einsum('cthd,cshd->chts', qf, kf)
    attn_weights = jnp.where(causal, scores, 0.0).astype(jnp.bfloat16).astype(jnp.float32)
    back_scores = jnp.where(causal, jnp.einsum('cthe,cshe->chts', gf, vf), 0.0).astype(jnp.bfloat16).astype(jnp.float32)
    d_query = jnp.einsum('chts,cshd->cthd', back_scores, kf) + jnp.einsum('cthe,chde->cthd', gf, cf)
    d_key = jnp.einsum('chts,cthd->cshd', back_scores, qf) + jnp.einsum('cshe,chde->cshd', vf, lf)
    d_value = jnp.einsum('chts,cthe->cshe', attn_weights, gf) + jnp.einsum('cshd,chde->cshe', kf, lf)
    return (d_query.astype(jnp.bfloat16), d_key.astype(jnp.bfloat16), d_value.astype(jnp.bfloat16))

def reference(tokens, w_query, w_key, w_value, w_output, out_cotangent):
    clip_count = tokens.shape[0]
    flattened = tokens.reshape(-1, D)
    queries = to_blocks(project(flattened, w_query).reshape(clip_count, LENGTH, D))
    key_rows = to_blocks(project(flattened, w_key).reshape(clip_count, LENGTH, D))
    value_rows = to_blocks(project(flattened, w_value).reshape(clip_count, LENGTH, D))
    states = jnp.einsum('bcshd,bcshe->bchde', key_rows.astype(jnp.float32), value_rows.astype(jnp.float32))
    zero_state = jnp.zeros_like(states[:1])
    carried = jnp.concatenate([zero_state, jnp.cumsum(states, axis=0)[:-1]], axis=0).astype(jnp.bfloat16)
    mixed = from_blocks(lax.map(forward_block, (queries, key_rows, value_rows, carried)))
    scale_rows = jnp.sqrt(lax.optimization_barrier(jnp.mean(mixed * mixed, axis=-1, keepdims=True)) + EPSILON)
    normed = mixed / scale_rows
    normed_bf = normed.astype(jnp.bfloat16)
    normed_flat = normed_bf.reshape(-1, D)
    attended = jnp.dot(normed_flat, w_output, preferred_element_type=jnp.float32).astype(jnp.bfloat16)
    attended = attended.reshape(clip_count, LENGTH, D)
    cot_flat = out_cotangent.reshape(-1, D)
    back_norm = jnp.dot(cot_flat, w_output.T, preferred_element_type=jnp.float32).reshape(clip_count, LENGTH, D)
    d_mixed = ((back_norm - normed * lax.optimization_barrier(jnp.mean(back_norm * normed, axis=-1, keepdims=True))) / scale_rows).astype(jnp.bfloat16)
    d_heads = to_blocks(d_mixed)
    back_states = jnp.einsum('bcthd,bcthe->bchde', queries.astype(jnp.float32), d_heads.astype(jnp.float32))
    reversed_sums = jnp.cumsum(back_states[::-1], axis=0)[::-1]
    later = jnp.concatenate([reversed_sums[1:], zero_state], axis=0).astype(jnp.bfloat16)
    d_query, d_key, d_value = lax.map(backward_block, (queries, key_rows, value_rows, carried, later, d_heads))
    d_query = from_blocks(d_query).reshape(-1, D)
    d_key = from_blocks(d_key).reshape(-1, D)
    d_value = from_blocks(d_value).reshape(-1, D)
    d_tokens = jnp.dot(d_query, w_query.T, preferred_element_type=jnp.float32)
    d_tokens = d_tokens + jnp.dot(d_key, w_key.T, preferred_element_type=jnp.float32)
    d_tokens = d_tokens + jnp.dot(d_value, w_value.T, preferred_element_type=jnp.float32)
    d_tokens = d_tokens.astype(jnp.bfloat16).reshape(clip_count, LENGTH, D)
    grad_query = jnp.dot(flattened.T, d_query, preferred_element_type=jnp.float32)
    grad_key = jnp.dot(flattened.T, d_key, preferred_element_type=jnp.float32)
    grad_value = jnp.dot(flattened.T, d_value, preferred_element_type=jnp.float32)
    grad_output = jnp.dot(normed_flat.T, cot_flat, preferred_element_type=jnp.float32)
    factor = 1.0 / math.sqrt(CLIPS * LENGTH)
    weight_grads = jnp.concatenate([grad_query, grad_key, grad_value, grad_output], axis=1) * factor
    return (attended, d_tokens, weight_grads)
```

```python
import functools
import math

import jax
import jax.numpy as jnp
from jax import lax
from jax.experimental import pallas as pl
from jax.experimental.pallas import tpu as pltpu
from jax.sharding import PartitionSpec as P

H = 8
EPSILON = 1e-05
PIECES = 4
F32, BF16 = jnp.float32, jnp.bfloat16
WHOLE = pl.BlockSpec(memory_space=pltpu.VMEM)


def call(body, info, outs, ins, scratch=(), name=None, flops=0):
    arrays, specs, moved = [], [], 0
    for entry in ins:
        if isinstance(entry, tuple):
            array, block, index = entry
            arrays.append(array)
            specs.append(pl.BlockSpec(block, index))
            moved += math.prod(block) * array.dtype.itemsize
        else:
            arrays.append(entry)
            specs.append(WHOLE)
            moved += entry.size * entry.dtype.itemsize
    shapes = [jax.ShapeDtypeStruct(shape, dtype) for shape, dtype in outs]
    moved += sum(math.prod(shape) * jnp.dtype(dtype).itemsize for shape, dtype in outs)
    return pl.pallas_call(
        body,
        name=name,
        out_shape=shapes,
        grid_spec=pltpu.PrefetchScalarGridSpec(
            num_scalar_prefetch=1,
            grid=(1,),
            in_specs=specs,
            out_specs=[WHOLE] * len(shapes),
            scratch_shapes=list(scratch),
        ),
        compiler_params=pltpu.CompilerParams(vmem_limit_bytes=40 * 2**20),
        cost_estimate=pl.CostEstimate(flops=flops, bytes_accessed=moved, transcendentals=0),
    )(info, *arrays)


def dot(a, b, over=(1, 0)):
    return lax.dot_general(
        a, b, (((over[0],), (over[1],)), ((), ())), preferred_element_type=F32
    )


def head(array, h, size):
    return array[:, h * size : (h + 1) * size]


def causal(info_ref, rows, count):
    seq = info_ref[0]

    def position(dim):
        at = lax.broadcasted_iota(jnp.int32, (count, count), dim)
        piece = jnp.bitwise_xor(at // rows, seq)
        return piece * rows + at % rows

    return position(0) >= position(1)


def across(ref, rows):
    order = [piece ^ 1 for piece in range(PIECES)]
    return jnp.concatenate([ref[piece * rows : (piece + 1) * rows] for piece in order], axis=0)


def project_body(size, info, first, second, w_q, w_k, w_v, *rest):
    if len(rest) == 6:
        before, q_out, k_out, v_out, state_out, rows_out = rest
    else:
        before = None
        q_out, k_out, v_out, state_out, rows_out = rest
    rows = jnp.concatenate([first[...].astype(BF16), second[...].astype(BF16)], axis=0)
    rows_out[...] = rows
    q_out[...] = dot(rows, w_q[...]).astype(BF16)
    keys = dot(rows, w_k[...]).astype(BF16)
    k_out[...] = keys
    values = dot(rows, w_v[...]).astype(BF16)
    v_out[...] = values
    for h in range(keys.shape[1] // size):
        state = dot(head(keys, h, size), head(values, h, size), (0, 0))
        if before is not None:
            state = state + before[h * size : (h + 1) * size]
        state_out[h * size : (h + 1) * size] = state


def inside_body(rows, size, info, q0, q1, k0, k1, v0, v1, c0, c1, c2, c3, w_o, *outs):
    q_out, k_out, v_out, attn_out, mixed_out, back_out, cot_out = outs
    q = jnp.concatenate([q0[...], q1[...]], axis=0)
    k = jnp.concatenate([k0[...], k1[...]], axis=0)
    v = jnp.concatenate([v0[...], v1[...]], axis=0)
    q_out[...], k_out[...], v_out[...] = q, k, v
    mask = causal(info, rows, q.shape[0])
    for h in range(q.shape[1] // size):
        scores = dot(head(q, h, size), head(k, h, size), (1, 1))
        attn = jnp.where(mask, scores, 0.0).astype(BF16)
        attn_out[h] = attn
        mixed_out[:, h * size : (h + 1) * size] = dot(attn, head(v, h, size))
    cot = jnp.concatenate([c[...].astype(BF16) for c in (c0, c1, c2, c3)], axis=0)
    cot_out[...] = cot
    back_out[...] = dot(cot, w_o[...], (1, 1))


def stats_body(size, info, q, carried, inner, back, mixed_out, stats_out):
    for h in range(q.shape[1] // size):
        state = carried[h * size : (h + 1) * size].astype(BF16)
        mixed_out[:, h * size : (h + 1) * size] = inner[:, h * size : (h + 1) * size] + dot(
            head(q, h, size), state
        )
    mixed = mixed_out[...]
    squares = jnp.sum(mixed * mixed, axis=1, keepdims=True)
    cross = jnp.sum(mixed * back[...], axis=1, keepdims=True)
    lane = lax.broadcasted_iota(jnp.int32, stats_out.shape, 1)
    stats_out[...] = jnp.where(lane == 0, squares, cross)


def norm_body(rows, size, width, info, q, mixed, back, mine, other, normed_out, d_out, state_out):
    total = mine[...] + across(other, rows)
    squares, cross = total[:, 0:1], total[:, 1:2]
    scale = jnp.sqrt(squares * (1.0 / width) + EPSILON)
    normed = mixed[...] / scale
    normed_out[...] = normed.astype(BF16).astype(F32)
    mean = cross / scale * (1.0 / width)
    d_mixed = ((back[...] - normed * mean) / scale).astype(BF16)
    d_out[...] = d_mixed
    for h in range(q.shape[1] // size):
        state_out[h * size : (h + 1) * size] = dot(head(q, h, size), head(d_mixed, h, size), (0, 0))


def back_body(rows, size, info, q, k, v, d_mixed, attn, carried, dq_out, dk_out, dv_out):
    mask = causal(info, rows, q.shape[0])
    for h in range(q.shape[1] // size):
        at = slice(h * size, (h + 1) * size)
        d_head = d_mixed[:, at]
        scores = dot(d_head, v[:, at], (1, 1))
        scores = jnp.where(mask, scores, 0.0).astype(BF16)
        state = carried[at].astype(BF16)
        dq_out[:, at] = (dot(scores, k[:, at]) + dot(d_head, state, (1, 1))).astype(BF16)
        dk_out[:, at] = dot(scores, q[:, at], (0, 0))
        dv_out[:, at] = dot(attn[h], d_head, (0, 0))


def finish_body(size, info, k, v, later, dk_in, dv_in, dk_out, dv_out):
    for h in range(k.shape[1] // size):
        at = slice(h * size, (h + 1) * size)
        state = later[at].astype(BF16)
        dk_out[:, at] = (dk_in[:, at] + dot(v[:, at], state, (1, 1))).astype(BF16)
        dv_out[:, at] = (dv_in[:, at] + dot(k[:, at], state)).astype(BF16)


def split_rows(info, n_seq, n_dp, total, keep_out, send_out):
    block = total.shape[0] // (n_seq * n_dp)
    kept = keep_out.shape[0] // block
    for slot in range(n_seq * n_dp):
        i, j = slot // n_seq, slot % n_seq
        owner = jnp.bitwise_xor(info[0], j) * n_dp + jnp.bitwise_xor(info[1], i)
        part = total[pl.ds(pl.multiple_of(owner * block, block), block), :]
        if slot < kept:
            keep_out[slot * block : (slot + 1) * block] = part
        else:
            send_out[(slot - kept) * block : (slot - kept + 1) * block] = part


def grad_body(n_seq, n_dp, factor, info, r0, r1, grad, keep_out, send_out, total):
    half = r0.shape[0]
    total[...] = (
        dot(r0[...], grad[:half], (0, 0)) + dot(r1[...], grad[half:], (0, 0))
    ) * factor
    split_rows(info, n_seq, n_dp, total, keep_out, send_out)


def grad_out_body(rows, n_seq, n_dp, factor, info, mine, other, cot, keep_out, send_out, total):
    half = mine.shape[1]
    core = info[2]
    for array, at in ((mine[...], core), (across(other, rows), 1 - core)):
        total[pl.ds(pl.multiple_of(at * half, half), half), :] = (
            dot(array.astype(BF16), cot[...], (0, 0)) * factor
        )
    split_rows(info, n_seq, n_dp, total, keep_out, send_out)


def attended_body(rows, info, mine, other, w_o, out):
    half = mine.shape[1]
    core = info[2]
    total = None
    for array, at in ((mine[:rows], core), (other[rows : 2 * rows], 1 - core)):
        weight = w_o[pl.ds(pl.multiple_of(at * half, half), half), :]
        part = dot(array.astype(BF16), weight)
        total = part if total is None else total + part
    out[...] = total.astype(BF16)


def tokens_body(rows, info, dq, dk, dv, w_q, w_k, w_v, mine_out, other_out):
    total = dot(dq[: 2 * rows], w_q[...], (1, 1))
    total = total + dot(dk[: 2 * rows], w_k[...], (1, 1))
    total = total + dot(dv[: 2 * rows], w_v[...], (1, 1))
    mine_out[...] = total[:rows]
    other_out[...] = total[rows:]


def assemble_body(width, info, *refs):
    out = refs[-1]
    block = refs[0].shape[1]
    for at, ref in enumerate(refs[:-1]):
        tensor, piece = at // PIECES, at % PIECES
        source = jnp.bitwise_xor(info[0], piece)
        column = tensor * width + (source % 2) * (width // 2) + (source // 2 % 2) * block
        out[:, pl.ds(pl.multiple_of(column, block), block)] = ref[...]


def partners(count, bit):
    return [(i, i ^ bit) for i in range(count)]


def local(tokens, w_query, w_key, w_value, w_output, out_cotangent):
    clip_count, rows, width = tokens.shape
    assert clip_count == 1
    size = width // H
    half = width // 2
    quarter = width // 4
    count = PIECES * rows
    n_seq, n_dp = lax.axis_size("seq"), lax.axis_size("dp")
    pairs = n_seq // PIECES
    seq, place = lax.axis_index("seq"), lax.axis_index("dp")
    core = seq % 2
    info = jnp.stack([seq, place, core, seq // 2 % 2]).astype(jnp.int32)
    swap = functools.partial(lax.ppermute, axis_name="seq")

    def gather(array):
        near = swap(array, perm=partners(n_seq, 1))
        far = swap(array, perm=partners(n_seq, 2))
        return near, far, swap(far, perm=partners(n_seq, 1))

    tok = tokens.reshape(rows, width)
    tok1, tok2, tok3 = gather(tok.astype(F32))
    cot = out_cotangent.reshape(rows, width)
    cot1, cot2, cot3 = gather(cot.astype(F32))

    columns = lambda i, info: (0, info[2])
    weights = [(w, (width, half), columns) for w in (w_query, w_key, w_value)]
    narrow = (2 * rows, half)
    outs = [(narrow, BF16)] * 3 + [((half, size), F32), ((2 * rows, width), BF16)]
    body = functools.partial(project_body, size)
    flops = 2 * 2 * rows * width * half * 3
    q0, k0, v0, state0, rows0 = call(body, info, outs, [tok, tok1, *weights], name="proj0", flops=flops)
    q1, k1, v1, state, rows1 = call(
        body, info, outs, [tok2, tok3, *weights, state0], name="proj1", flops=flops
    )

    def arriving(value, forward):
        total = None
        for d in range(1, pairs):
            shift = PIECES * d
            links = [(i, i + shift) for i in range(n_seq - shift)]
            if not forward:
                links = [(j, i) for i, j in links]
            got = swap(value, perm=links)
            total = got if total is None else total + got
        return total

    carried = arriving(state, True)
    wide = (count, half)
    q, k, v, attn, inner, back, cot_all = call(
        functools.partial(inside_body, rows, size),
        info,
        [(wide, BF16)] * 3
        + [((H // 2, count, count), BF16), (wide, F32), (wide, F32), ((count, width), BF16)],
        [q0, q1, k0, k1, v0, v1, cot, cot1, cot2, cot3, (w_output, (half, width), lambda i, info: (info[2], 0))],
        name="inside",
        flops=2 * count * width * half + 4 * 4 * count * count * size,
    )
    mixed, stats = call(
        functools.partial(stats_body, size),
        info,
        [(wide, F32), ((count, 128), F32)],
        [q, carried, inner, back],
        name="stats",
        flops=2 * count * half * size,
    )
    stats_other = swap(stats, perm=partners(n_seq, 1))
    normed, d_mixed, own_back = call(
        functools.partial(norm_body, rows, size, width),
        info,
        [(wide, F32), (wide, BF16), ((half, size), F32)],
        [q, mixed, back, stats, stats_other],
        name="norm",
        flops=2 * count * half * size,
    )
    later = arriving(own_back, False)
    normed_other = swap(normed, perm=partners(n_seq, 1))
    dq, dk_inner, dv_inner = call(
        functools.partial(back_body, rows, size),
        info,
        [(wide, BF16), (wide, F32), (wide, F32)],
        [q, k, v, d_mixed, attn, carried],
        name="back",
        flops=8 * 4 * count * count * size,
    )

    factor = 1.0 / math.sqrt(clip_count * n_dp * rows * n_seq)
    chunk = [((width // 2, quarter), F32)] * 2
    scratch = [pltpu.VMEM((width, quarter), F32)]
    grad_flops = 2 * count * width * quarter

    def reduce_rows(keep, send):
        bit = n_dp // 2
        while bit:
            keep = keep + lax.ppermute(send, "dp", partners(n_dp, bit))
            bit //= 2
            if bit:
                middle = keep.shape[0] // 2
                keep, send = keep[:middle], keep[middle:]
        bit = n_seq // 2
        while bit >= PIECES:
            middle = keep.shape[0] // 2
            keep = keep[:middle] + swap(keep[middle:], perm=partners(n_seq, bit))
            bit //= 2
        block = keep.shape[0] // PIECES
        parts = [keep[i * block : (i + 1) * block] for i in range(PIECES)]
        return parts[:1] + [swap(parts[i], perm=partners(n_seq, i)) for i in range(1, PIECES)]

    def weight_grad(grad, name):
        return call(
            functools.partial(grad_body, n_seq, n_dp, factor),
            info,
            chunk,
            [rows0, rows1, (grad, (count, quarter), lambda i, info: (0, info[3]))],
            scratch,
            name=name,
            flops=grad_flops,
        )

    parts_q = reduce_rows(*weight_grad(dq, "grad_q"))
    parts_o = reduce_rows(
        *call(
            functools.partial(grad_out_body, rows, n_seq, n_dp, factor),
            info,
            chunk,
            [normed, normed_other, (cot_all, (count, quarter), lambda i, info: (0, 2 * info[2] + info[3]))],
            scratch,
            name="grad_o",
            flops=grad_flops,
        )
    )
    (attended,) = call(
        functools.partial(attended_body, rows),
        info,
        [((rows, width), BF16)],
        [normed, normed_other, w_output],
        name="attended",
        flops=2 * rows * width * width,
    )
    dk, dv = call(
        functools.partial(finish_body, size),
        info,
        [(wide, BF16)] * 2,
        [k, v, later, dk_inner, dv_inner],
        name="finish",
        flops=4 * count * half * size,
    )
    parts_k = reduce_rows(*weight_grad(dk, "grad_k"))
    parts_v = reduce_rows(*weight_grad(dv, "grad_v"))
    mine, other = call(
        functools.partial(tokens_body, rows),
        info,
        [((rows, width), F32)] * 2,
        [dq, dk, dv, *weights],
        name="d_tokens",
        flops=6 * 2 * rows * width * half,
    )
    d_tokens = (mine + swap(other, perm=partners(n_seq, 1))).astype(BF16)
    (grads,) = call(
        functools.partial(assemble_body, width),
        info,
        [((width // (n_seq * n_dp), 4 * width), F32)],
        parts_q + parts_k + parts_v + parts_o,
        name="assemble",
    )
    return (
        attended.reshape(tokens.shape),
        d_tokens.reshape(tokens.shape),
        grads,
    )


def solution(mesh):
    return jax.shard_map(
        local,
        mesh=mesh,
        in_specs=(
            P(("groups", "dp"), "seq", None),
            P(),
            P(),
            P(),
            P(),
            P(("groups", "dp"), "seq", None),
        ),
        out_specs=(
            P(("groups", "dp"), "seq", None),
            P(("groups", "dp"), "seq", None),
            P(("groups", "seq", "dp"), None),
        ),
        check_vma=False,
    )
```

```python
import functools
import math

import jax
import jax.numpy as jnp
from jax import lax
from jax.experimental import pallas as pl
from jax.experimental.pallas import tpu as pltpu
from jax.sharding import PartitionSpec as P

H = 8
LAG, WINDOW, AHEAD = 2.5, 2, 2
EPSILON = 1e-05
PIECES = 4
F32, BF16 = jnp.float32, jnp.bfloat16
WHOLE = pl.BlockSpec(memory_space=pltpu.VMEM)


def call(body, info, outs, ins, scratch=(), name=None, flops=0):
    arrays, specs, moved = [], [], 0
    for entry in ins:
        if isinstance(entry, tuple):
            array, block, index = entry
            arrays.append(array)
            specs.append(pl.BlockSpec(block, index))
            moved += math.prod(block) * array.dtype.itemsize
        else:
            arrays.append(entry)
            specs.append(WHOLE)
            moved += entry.size * entry.dtype.itemsize
    shapes = [jax.ShapeDtypeStruct(shape, dtype) for shape, dtype in outs]
    moved += sum(math.prod(shape) * jnp.dtype(dtype).itemsize for shape, dtype in outs)
    return pl.pallas_call(
        body,
        name=name,
        out_shape=shapes,
        grid_spec=pltpu.PrefetchScalarGridSpec(
            num_scalar_prefetch=1,
            grid=(1,),
            in_specs=specs,
            out_specs=[WHOLE] * len(shapes),
            scratch_shapes=list(scratch),
        ),
        compiler_params=pltpu.CompilerParams(vmem_limit_bytes=24 * 2**20),
        cost_estimate=pl.CostEstimate(flops=1, bytes_accessed=1, transcendentals=0),
    )(info, *arrays)


def dot(a, b, over=(1, 0)):
    return lax.dot_general(
        a, b, (((over[0],), (over[1],)), ((), ())), preferred_element_type=F32
    )


def head(array, h, size):
    return array[:, h * size : (h + 1) * size]


def causal(info_ref, rows, count):
    seq = info_ref[0]

    def position(dim):
        at = lax.broadcasted_iota(jnp.int32, (count, count), dim)
        piece = jnp.bitwise_xor(at // rows, seq)
        return piece * rows + at % rows

    return position(0) >= position(1)


def across(ref, rows):
    order = [piece ^ 1 for piece in range(PIECES)]
    return jnp.concatenate([ref[piece * rows : (piece + 1) * rows] for piece in order], axis=0)


def project_body(n_seq, size, info, first, second, w_q, w_k, w_v, *rest):
    if len(rest) == 6:
        before, q_out, k_out, v_out, state_out, rows_out = rest
    else:
        before = None
        q_out, k_out, v_out, state_out, rows_out = rest
    width = first.shape[1]
    rows = jnp.concatenate([first[...].astype(BF16), second[...].astype(BF16)], axis=0)
    block = 2 * width // n_seq
    for pair in range(n_seq // PIECES):
        at = pl.ds(pl.multiple_of((pair * 2 + info[3]) * block, block), block)
        for i, ref in enumerate((first, second)):
            count = ref.shape[0]
            rows_out[i * count : (i + 1) * count, pair * block : (pair + 1) * block] = ref[:, at].astype(BF16)
    q_out[...] = dot(rows, w_q[...]).astype(BF16)
    keys = dot(rows, w_k[...]).astype(BF16)
    k_out[...] = keys
    values = dot(rows, w_v[...]).astype(BF16)
    v_out[...] = values
    for h in range(keys.shape[1] // size):
        state = dot(head(keys, h, size), head(values, h, size), (0, 0))
        if before is not None:
            state = state + before[h * size : (h + 1) * size]
        state_out[h * size : (h + 1) * size] = state


def inside_body(rows, size, info, q0, q1, k0, k1, v0, v1, *outs):
    q_out, k_out, v_out, attn_out, mixed_out = outs
    q = jnp.concatenate([q0[...], q1[...]], axis=0)
    k = jnp.concatenate([k0[...], k1[...]], axis=0)
    v = jnp.concatenate([v0[...], v1[...]], axis=0)
    q_out[...], k_out[...], v_out[...] = q, k, v
    mask = causal(info, rows, q.shape[0])
    for h in range(q.shape[1] // size):
        scores = dot(head(q, h, size), head(k, h, size), (1, 1))
        attn = jnp.where(mask, scores, 0.0).astype(BF16)
        attn_out[h] = attn
        mixed_out[:, h * size : (h + 1) * size] = dot(attn, head(v, h, size))


def cotangent_body(info, c0, c1, c2, c3, w_o, cot_out, back_out):
    cot = jnp.concatenate([c[...].astype(BF16) for c in (c0, c1, c2, c3)], axis=0)
    cot_out[...] = cot
    back_out[...] = dot(cot, w_o[...], (1, 1))


def stats_body(size, info, q, carried, inner, back, mixed_out, stats_out):
    for h in range(q.shape[1] // size):
        state = carried[h * size : (h + 1) * size].astype(BF16)
        mixed_out[:, h * size : (h + 1) * size] = inner[:, h * size : (h + 1) * size] + dot(
            head(q, h, size), state
        )
    mixed = mixed_out[...]
    squares = jnp.sum(mixed * mixed, axis=1, keepdims=True)
    cross = jnp.sum(mixed * back[...], axis=1, keepdims=True)
    lane = lax.broadcasted_iota(jnp.int32, stats_out.shape, 1)
    stats_out[...] = jnp.where(lane == 0, squares, cross)


def norm_body(rows, size, width, info, q, mixed, back, mine, other, normed_out, d_out, state_out):
    total = mine[...] + across(other, rows)
    squares, cross = total[:, 0:1], total[:, 1:2]
    scale = jnp.sqrt(squares * (1.0 / width) + EPSILON)
    normed = mixed[...] / scale
    normed_out[...] = normed.astype(BF16).astype(F32)
    mean = cross / scale * (1.0 / width)
    d_mixed = ((back[...] - normed * mean) / scale).astype(BF16)
    d_out[...] = d_mixed
    for h in range(q.shape[1] // size):
        state_out[h * size : (h + 1) * size] = dot(head(q, h, size), head(d_mixed, h, size), (0, 0))


def back_query_body(rows, size, info, k, v, d_mixed, carried, dq_out, scores_out):
    mask = causal(info, rows, k.shape[0])
    for h in range(k.shape[1] // size):
        at = slice(h * size, (h + 1) * size)
        d_head = d_mixed[:, at]
        scores = dot(d_head, v[:, at], (1, 1))
        scores = jnp.where(mask, scores, 0.0).astype(BF16)
        state = carried[at].astype(BF16)
        scores_out[h] = scores
        dq_out[:, at] = (dot(scores, k[:, at]) + dot(d_head, state, (1, 1))).astype(BF16)


def back_rest_body(size, info, q, d_mixed, attn, scores, dk_out, dv_out):
    for h in range(q.shape[1] // size):
        at = slice(h * size, (h + 1) * size)
        dk_out[:, at] = dot(scores[h], q[:, at], (0, 0))
        dv_out[:, at] = dot(attn[h], d_mixed[:, at], (0, 0))


def finish_body(size, info, k, v, later, dk_in, dv_in, dk_out, dv_out):
    for h in range(k.shape[1] // size):
        at = slice(h * size, (h + 1) * size)
        state = later[at].astype(BF16)
        dk_out[:, at] = (dk_in[:, at] + dot(v[:, at], state, (1, 1))).astype(BF16)
        dv_out[:, at] = (dv_in[:, at] + dot(k[:, at], state)).astype(BF16)


def split_rows(info, pairs, n_dp, total, *outs):
    keep_outs, send_outs = outs[: len(outs) // 2], outs[len(outs) // 2 :]
    columns = keep_outs[0].shape[1]
    kept = keep_outs[0].shape[0]
    block = total.shape[0] // (pairs * 2 * n_dp)
    seq, place = info[0], info[1]
    for slot in range(pairs * 2 * n_dp):
        i, pair, core = slot // (2 * pairs), slot // 2 % pairs, slot % 2
        owner = jnp.bitwise_xor(seq // PIECES, pair) * 2 + jnp.bitwise_xor(seq % 2, core)
        owner = owner * n_dp + jnp.bitwise_xor(place, i)
        rows = pl.ds(pl.multiple_of(owner * block, block), block)
        at = slot * block
        targets = keep_outs if at < kept else send_outs
        at = at % kept
        for chunk, target in enumerate(targets):
            target[at : at + block] = total[rows, chunk * columns : (chunk + 1) * columns]


def grad_body(pairs, n_dp, factor, info, r0, r1, grad, *outs):
    outs, total = outs[:-1], outs[-1]
    half = r0.shape[0]
    total[...] = (
        dot(r0[...], grad[:half], (0, 0)) + dot(r1[...], grad[half:], (0, 0))
    ) * factor
    split_rows(info, pairs, n_dp, total, *outs)


def grad_out_body(rows, pairs, n_dp, factor, info, mine, other, cot, *outs):
    outs, total = outs[:-1], outs[-1]
    core, chip = info[2], info[3]
    block = 2 * mine.shape[1] // (2 * pairs)
    per_core = mine.shape[1] // block
    order = [piece ^ 1 for piece in range(PIECES)]
    for pair in range(pairs):
        index = pair * 2 + chip
        at = pl.ds(pl.multiple_of(index % per_core * block, block), block)
        is_mine = index // per_core == core
        parts = [
            jnp.where(is_mine, mine[p * rows : (p + 1) * rows, at], other[order[p] * rows : (order[p] + 1) * rows, at])
            for p in range(PIECES)
        ]
        left = jnp.concatenate(parts, axis=0).astype(BF16)
        total[pair * block : (pair + 1) * block] = dot(left, cot[...], (0, 0)) * factor
    split_rows(info, pairs, n_dp, total, *outs)


def attended_body(rows, info, mine, other, w_o, out):
    half = mine.shape[1]
    core = info[2]
    total = None
    for array, at in ((mine[:rows], core), (other[rows : 2 * rows], 1 - core)):
        weight = w_o[pl.ds(pl.multiple_of(at * half, half), half), :]
        part = dot(array.astype(BF16), weight)
        total = part if total is None else total + part
    out[...] = total.astype(BF16)


def tokens_body(rows, info, dq, dk, dv, w_q, w_k, w_v, mine_out, other_out):
    total = dot(dq[: 2 * rows], w_q[...], (1, 1))
    total = total + dot(dk[: 2 * rows], w_k[...], (1, 1))
    total = total + dot(dv[: 2 * rows], w_v[...], (1, 1))
    mine_out[...] = total[:rows]
    other_out[...] = total[rows:]


def assemble_body(width, chunks, order, info, *refs):
    pieces, others, out = refs[:-2], refs[-2], refs[-1]
    rows, block = pieces[0].shape
    for at, ref in enumerate(pieces):
        start = order[at // chunks] * width + at % chunks * block
        for core, part in ((info[2], ref[...]), (1 - info[2], others[at * rows : (at + 1) * rows])):
            column = pl.multiple_of(start + core * (width // 2), block)
            out[:, pl.ds(column, block)] = part


def after(value, *others):
    return lax.optimization_barrier((value, *others))[0]


def partners(count, bit):
    return [(i, i ^ bit) for i in range(count)]


def local(tokens, w_query, w_key, w_value, w_output, out_cotangent):
    clip_count, rows, width = tokens.shape
    assert clip_count == 1
    size = width // H
    half = width // 2
    count = PIECES * rows
    n_seq, n_dp = lax.axis_size("seq"), lax.axis_size("dp")
    pairs = n_seq // PIECES
    seq, place = lax.axis_index("seq"), lax.axis_index("dp")
    info = jnp.stack([seq, place, seq % 2, seq // 2 % 2]).astype(jnp.int32)
    swap = functools.partial(lax.ppermute, axis_name="seq")
    core_links, chip_links = partners(n_seq, 1), partners(n_seq, 2)

    def shift(value, forward):
        total = None
        for d in range(1, pairs):
            links = [(i, i + PIECES * d) for i in range(n_seq - PIECES * d)]
            if not forward:
                links = [(j, i) for i, j in links]
            got = swap(value, perm=links)
            total = got if total is None else total + got
        return total

    tok = tokens.reshape(rows, width)
    cot = out_cotangent.reshape(rows, width)
    tok_f32 = tok.astype(F32)
    tok2 = swap(tok_f32, perm=chip_links)
    tok1 = swap(tok_f32, perm=core_links)
    cot_f32 = after(cot, tok_f32).astype(F32)
    cot2 = swap(cot_f32, perm=chip_links)
    cot1 = swap(cot_f32, perm=core_links)

    columns = lambda i, info: (0, info[2])
    weights = [(w, (width, half), columns) for w in (w_query, w_key, w_value)]
    narrow, wide = (2 * rows, half), (count, half)
    outs = [(narrow, BF16)] * 3 + [((half, size), F32), (narrow, BF16)]
    body = functools.partial(project_body, n_seq, size)
    flops = 2 * 2 * rows * width * half * 3
    q0, k0, v0, state0, rows0 = call(body, info, outs, [tok, tok1, *weights], name="proj0", flops=flops)
    tok2 = after(tok2, state0)
    tok3 = swap(tok2, perm=core_links)
    q1, k1, v1, state, rows1 = call(
        body, info, outs, [tok2, tok3, *weights, state0], name="proj1", flops=flops
    )
    carried = shift(state, True)
    q, k, v, attn, inner = call(
        functools.partial(inside_body, rows, size),
        info,
        [(wide, BF16)] * 3 + [((H // 2, count, count), BF16), (wide, F32)],
        [q0, q1, k0, k1, v0, v1],
        name="inside",
        flops=4 * 4 * count * count * size,
    )
    cot2 = after(cot2, carried, inner)
    cot3 = swap(cot2, perm=core_links)
    cot_all, back = call(
        cotangent_body,
        info,
        [((count, width), BF16), (wide, F32)],
        [cot, cot1, cot2, cot3, (w_output, (half, width), lambda i, info: (info[2], 0))],
        name="cotangent",
        flops=2 * count * width * half,
    )
    carried = after(carried, back, inner)
    mixed, stats = call(
        functools.partial(stats_body, size),
        info,
        [(wide, F32), ((count, 128), F32)],
        [q, carried, inner, back],
        name="stats",
        flops=2 * count * half * size,
    )
    stats_other = swap(stats, perm=core_links)
    normed, d_mixed, own_back = call(
        functools.partial(norm_body, rows, size, width),
        info,
        [(wide, F32), (wide, BF16), ((half, size), F32)],
        [q, mixed, back, stats, stats_other],
        name="norm",
        flops=2 * count * half * size,
    )
    later = shift(own_back, False)
    normed_other = swap(normed, perm=core_links)
    dq, back_scores = call(
        functools.partial(back_query_body, rows, size),
        info,
        [(wide, BF16), ((H // 2, count, count), BF16)],
        [k, v, d_mixed, carried],
        name="back_query",
        flops=4 * 4 * count * count * size,
    )

    factor = 1.0 / math.sqrt(clip_count * n_dp * rows * n_seq)
    chunks = 2
    chunk = [((half // 2, half // chunks), F32)] * (2 * chunks)
    scratch = [pltpu.VMEM((half, half), F32)]
    grad_flops = 2 * count * half * half

    hops = []
    bit = n_dp // 2
    while bit:
        hops.append(("dp", partners(n_dp, bit)))
        bit //= 2
    bit = n_seq // 2
    while bit >= PIECES:
        hops.append(("seq", partners(n_seq, bit)))
        bit //= 2

    def reduce_all(tensors, fillers):
        total_chunks = len(tensors) * chunks
        keeps, sends, made = {}, {}, {}
        steps = [(p + LAG * hop, hop, p) for p in range(total_chunks) for hop in range(len(hops))]
        last, first_hop = None, {}
        for at, (_, hop, p) in enumerate(sorted(steps)):
            for n in range(len(tensors)):
                if n not in made and chunks * n <= (p if hop == 0 else 0) + AHEAD:
                    made[n] = tensors[n](last)
                    for c in range(chunks):
                        keeps[n * chunks + c] = made[n][c]
                        sends[n * chunks + c] = made[n][chunks + c]
            axis, links = hops[hop]
            if hop == 0 and p - WINDOW in first_hop:
                sends[p] = after(sends[p], first_hop[p - WINDOW])
            if at in fillers:
                last = fillers[at](last)
            got = lax.ppermute(sends[p], axis, links)
            total = (keeps[p] if last is None else after(keeps[p], last)) + got
            last = total
            if hop == 0:
                first_hop[p] = total
            middle = total.shape[0] // 2
            keeps[p], sends[p] = total[:middle], total[middle:]
        out = [keeps[p] for p in range(total_chunks)]
        return out, swap(jnp.concatenate([sends[p] for p in range(total_chunks)]), perm=core_links)

    def weight_grad(grad, name):
        return call(
            functools.partial(grad_body, pairs, n_dp, factor),
            info,
            chunk,
            [rows0, rows1, grad],
            scratch,
            name=name,
            flops=grad_flops,
        )

    results = {}

    def grad_query(last):
        return weight_grad(dq, "grad_q")

    def grad_output(last):
        return call(
            functools.partial(grad_out_body, rows, pairs, n_dp, factor),
            info,
            chunk,
            [normed, normed_other, (cot_all, (count, half), columns)],
            scratch,
            name="grad_o",
            flops=grad_flops,
        )

    def grad_key(last):
        dk_inner, dv_inner = call(
            functools.partial(back_rest_body, size),
            info,
            [(wide, F32), (wide, F32)],
            [q, d_mixed, attn, after(back_scores, normed_other)],
            name="back_rest",
            flops=4 * 4 * count * count * size,
        )
        results["dk"], results["dv"] = call(
            functools.partial(finish_body, size),
            info,
            [(wide, BF16)] * 2,
            [k, v, after(later, last), dk_inner, dv_inner],
            name="finish",
            flops=4 * count * half * size,
        )
        results["key"] = weight_grad(results["dk"], "grad_k")
        return results["key"]

    def grad_value(last):
        return weight_grad(after(results["dv"], results["key"][0]), "grad_v")


    def attend(last):
        (results["attended"],) = call(
            functools.partial(attended_body, rows),
            info,
            [((rows, width), BF16)],
            [after(normed, last), normed_other, w_output],
            name="attended",
            flops=2 * rows * width * width,
        )
        return results["attended"]

    def back_tokens(last):
        results["mine"], results["other"] = call(
            functools.partial(tokens_body, rows),
            info,
            [((rows, width), F32)] * 2,
            [after(dq, last), results["dk"], results["dv"], *weights],
            name="d_tokens",
            flops=6 * 2 * rows * width * half,
        )
        return results["mine"]

    own, other_core = reduce_all(
        [grad_query, grad_output, grad_key, grad_value], {4: attend, 7: back_tokens}
    )
    attended, mine, other = results["attended"], results["mine"], results["other"]
    d_tokens = (mine + swap(other, perm=core_links)).astype(BF16)
    (grads,) = call(
        functools.partial(assemble_body, width, chunks, (0, 3, 1, 2)),
        info,
        [((width // (n_seq * n_dp), 4 * width), F32)],
        own + [other_core],
        name="assemble",
    )
    return (
        attended.reshape(tokens.shape),
        d_tokens.reshape(tokens.shape),
        grads,
    )


def solution(mesh):
    return jax.shard_map(
        local,
        mesh=mesh,
        in_specs=(
            P(("groups", "dp"), "seq", None),
            P(),
            P(),
            P(),
            P(),
            P(("groups", "dp"), "seq", None),
        ),
        out_specs=(
            P(("groups", "dp"), "seq", None),
            P(("groups", "dp"), "seq", None),
            P(("groups", "seq", "dp"), None),
        ),
        check_vma=False,
    )
```

```python
import functools
import math

import jax
import jax.numpy as jnp
from jax import lax
from jax.experimental import pallas as pl
from jax.experimental.pallas import tpu as pltpu
from jax.sharding import PartitionSpec as P

H = 8
WINDOW, AHEAD = 3, 2
LAG = 1.5
WIDTHS = ((256, 256), (512,), (512,), (256, 256))
EPSILON = 1e-05
PIECES = 4
F32, BF16 = jnp.float32, jnp.bfloat16
WHOLE = pl.BlockSpec(memory_space=pltpu.VMEM)


def call(body, info, outs, ins, scratch=(), name=None, flops=0):
    arrays, specs, moved = [], [], 0
    for entry in ins:
        if isinstance(entry, tuple):
            array, block, index = entry
            arrays.append(array)
            specs.append(pl.BlockSpec(block, index))
            moved += math.prod(block) * array.dtype.itemsize
        else:
            arrays.append(entry)
            specs.append(WHOLE)
            moved += entry.size * entry.dtype.itemsize
    shapes = [jax.ShapeDtypeStruct(shape, dtype) for shape, dtype in outs]
    moved += sum(math.prod(shape) * jnp.dtype(dtype).itemsize for shape, dtype in outs)
    return pl.pallas_call(
        body,
        name=name,
        out_shape=shapes,
        grid_spec=pltpu.PrefetchScalarGridSpec(
            num_scalar_prefetch=1,
            grid=(1,),
            in_specs=specs,
            out_specs=[WHOLE] * len(shapes),
            scratch_shapes=list(scratch),
        ),
        compiler_params=pltpu.CompilerParams(vmem_limit_bytes=24 * 2**20),
        cost_estimate=pl.CostEstimate(flops=1, bytes_accessed=1, transcendentals=0),
    )(info, *arrays)


def dot(a, b, over=(1, 0)):
    return lax.dot_general(
        a, b, (((over[0],), (over[1],)), ((), ())), preferred_element_type=F32
    )


def head(array, h, size):
    return array[:, h * size : (h + 1) * size]


def causal(info_ref, rows, count):
    seq = info_ref[0]

    def position(dim):
        at = lax.broadcasted_iota(jnp.int32, (count, count), dim)
        piece = jnp.bitwise_xor(at // rows, seq)
        return piece * rows + at % rows

    return position(0) >= position(1)


def across(ref, rows):
    order = [piece ^ 1 for piece in range(PIECES)]
    return jnp.concatenate([ref[piece * rows : (piece + 1) * rows] for piece in order], axis=0)


def project_body(n_seq, size, info, first, second, w_q, w_k, w_v, *rest):
    if len(rest) == 6:
        before, q_out, k_out, v_out, state_out, rows_out = rest
    else:
        before = None
        q_out, k_out, v_out, state_out, rows_out = rest
    width = first.shape[1]
    rows = jnp.concatenate([first[...].astype(BF16), second[...].astype(BF16)], axis=0)
    block = 2 * width // n_seq
    for pair in range(n_seq // PIECES):
        at = pl.ds(pl.multiple_of((pair * 2 + info[3]) * block, block), block)
        for i, ref in enumerate((first, second)):
            count = ref.shape[0]
            rows_out[i * count : (i + 1) * count, pair * block : (pair + 1) * block] = ref[:, at].astype(BF16)
    q_out[...] = dot(rows, w_q[...]).astype(BF16)
    keys = dot(rows, w_k[...]).astype(BF16)
    k_out[...] = keys
    values = dot(rows, w_v[...]).astype(BF16)
    v_out[...] = values
    for h in range(keys.shape[1] // size):
        state = dot(head(keys, h, size), head(values, h, size), (0, 0))
        if before is not None:
            state = state + before[h * size : (h + 1) * size]
        state_out[h * size : (h + 1) * size] = state


def inside_body(rows, size, info, q0, q1, k0, k1, v0, v1, *outs):
    q_out, k_out, v_out, attn_out, mixed_out = outs
    q = jnp.concatenate([q0[...], q1[...]], axis=0)
    k = jnp.concatenate([k0[...], k1[...]], axis=0)
    v = jnp.concatenate([v0[...], v1[...]], axis=0)
    q_out[...], k_out[...], v_out[...] = q, k, v
    mask = causal(info, rows, q.shape[0])
    for h in range(q.shape[1] // size):
        scores = dot(head(q, h, size), head(k, h, size), (1, 1))
        attn = jnp.where(mask, scores, 0.0).astype(BF16)
        attn_out[h] = attn
        mixed_out[:, h * size : (h + 1) * size] = dot(attn, head(v, h, size))


def cotangent_body(info, c0, c1, c2, c3, w_o, cot_out, back_out):
    cot = jnp.concatenate([c[...].astype(BF16) for c in (c0, c1, c2, c3)], axis=0)
    cot_out[...] = cot
    back_out[...] = dot(cot, w_o[...], (1, 1))


def stats_body(size, info, q, carried, inner, back, mixed_out, stats_out):
    for h in range(q.shape[1] // size):
        state = carried[h * size : (h + 1) * size].astype(BF16)
        mixed_out[:, h * size : (h + 1) * size] = inner[:, h * size : (h + 1) * size] + dot(
            head(q, h, size), state
        )
    mixed = mixed_out[...]
    squares = jnp.sum(mixed * mixed, axis=1, keepdims=True)
    cross = jnp.sum(mixed * back[...], axis=1, keepdims=True)
    lane = lax.broadcasted_iota(jnp.int32, stats_out.shape, 1)
    stats_out[...] = jnp.where(lane == 0, squares, cross)


def norm_body(rows, size, pairs, n_dp, factor, info, q, k, v, mixed, back, mine, other, carried, r0, r1, *refs):
    normed_out, d_out, state_out, dq_out, scores_out = refs[:5]
    outs, total = refs[5:-1], refs[-1]
    width = 2 * mixed.shape[1]
    sums = mine[...] + across(other, rows)
    squares, cross = sums[:, 0:1], sums[:, 1:2]
    scale = jnp.sqrt(squares * (1.0 / width) + EPSILON)
    normed = mixed[...] / scale
    normed_out[...] = normed.astype(BF16).astype(F32)
    mean = cross / scale * (1.0 / width)
    d_mixed = ((back[...] - normed * mean) / scale).astype(BF16)
    d_out[...] = d_mixed
    mask = causal(info, rows, q.shape[0])
    heads = q.shape[1] // size
    states = []
    for h in range(heads):
        at = slice(h * size, (h + 1) * size)
        d_head = d_mixed[:, at]
        states.append(dot(q[:, at], d_head, (0, 0)))
        scores = dot(d_head, v[:, at], (1, 1))
        scores = jnp.where(mask, scores, 0.0).astype(BF16)
        scores_out[h] = scores
        state = carried[at].astype(BF16)
        dq_out[:, at] = (dot(scores, k[:, at]) + dot(d_head, state, (1, 1))).astype(BF16)
    for h in range(heads // 2):
        state_out[h * size : (h + 1) * size] = jnp.where(
            info[3] == 0, states[h], states[heads // 2 + h]
        )
    half = r0.shape[0]
    total[...] = (
        dot(r0[...], dq_out[:half], (0, 0)) + dot(r1[...], dq_out[half:], (0, 0))
    ) * factor
    split_rows(info, pairs, n_dp, total, *outs)


def back_rest_body(size, info, q, d_mixed, attn, scores, dk_out, dv_out):
    for h in range(q.shape[1] // size):
        at = slice(h * size, (h + 1) * size)
        dk_out[:, at] = dot(scores[h], q[:, at], (0, 0))
        dv_out[:, at] = dot(attn[h], d_mixed[:, at], (0, 0))


def finish_body(size, info, k, v, later, later_other, dk_in, dv_in, dk_out, dv_out):
    heads = k.shape[1] // size
    for h in range(heads):
        at = slice(h * size, (h + 1) * size)
        half = slice(h % (heads // 2) * size, (h % (heads // 2) + 1) * size)
        is_mine = info[3] == h // (heads // 2)
        state = jnp.where(is_mine, later[half], later_other[half]).astype(BF16)
        dk_out[:, at] = (dk_in[:, at] + dot(v[:, at], state, (1, 1))).astype(BF16)
        dv_out[:, at] = (dv_in[:, at] + dot(k[:, at], state)).astype(BF16)


def split_rows(info, pairs, n_dp, total, *outs):
    keep_outs, send_outs = outs[: len(outs) // 2], outs[len(outs) // 2 :]
    kept = keep_outs[0].shape[0]
    block = total.shape[0] // (pairs * 2 * n_dp)
    seq, place = info[0], info[1]
    for slot in range(pairs * 2 * n_dp):
        i, pair, core = slot // (2 * pairs), slot // 2 % pairs, slot % 2
        owner = jnp.bitwise_xor(seq // PIECES, pair) * 2 + jnp.bitwise_xor(seq % 2, core)
        owner = owner * n_dp + jnp.bitwise_xor(place, i)
        rows = pl.ds(pl.multiple_of(owner * block, block), block)
        at = slot * block
        targets = keep_outs if at < kept else send_outs
        at = at % kept
        start = 0
        for target in targets:
            target[at : at + block] = total[rows, start : start + target.shape[1]]
            start += target.shape[1]


def grad_body(pairs, n_dp, factor, info, r0, r1, grad, *outs):
    outs, total = outs[:-1], outs[-1]
    half = r0.shape[0]
    total[...] = (
        dot(r0[...], grad[:half], (0, 0)) + dot(r1[...], grad[half:], (0, 0))
    ) * factor
    split_rows(info, pairs, n_dp, total, *outs)


def grad_out_body(rows, pairs, n_dp, factor, info, mine, other, cot, *outs):
    outs, total = outs[:-1], outs[-1]
    core, chip = info[2], info[3]
    block = 2 * mine.shape[1] // (2 * pairs)
    per_core = mine.shape[1] // block
    order = [piece ^ 1 for piece in range(PIECES)]
    for pair in range(pairs):
        index = pair * 2 + chip
        at = pl.ds(pl.multiple_of(index % per_core * block, block), block)
        is_mine = index // per_core == core
        parts = [
            jnp.where(is_mine, mine[p * rows : (p + 1) * rows, at], other[order[p] * rows : (order[p] + 1) * rows, at])
            for p in range(PIECES)
        ]
        left = jnp.concatenate(parts, axis=0).astype(BF16)
        total[pair * block : (pair + 1) * block] = dot(left, cot[...], (0, 0)) * factor
    split_rows(info, pairs, n_dp, total, *outs)


def attended_body(rows, info, mine, other, w_o, out):
    half = mine.shape[1]
    core = info[2]
    total = None
    for array, at in ((mine[:rows], core), (other[rows : 2 * rows], 1 - core)):
        weight = w_o[pl.ds(pl.multiple_of(at * half, half), half), :]
        part = dot(array.astype(BF16), weight)
        total = part if total is None else total + part
    out[...] = total.astype(BF16)


def tokens_body(rows, info, dq, dk, dv, w_q, w_k, w_v, mine_out, other_out):
    total = dot(dq[: 2 * rows], w_q[...], (1, 1))
    total = total + dot(dk[: 2 * rows], w_k[...], (1, 1))
    total = total + dot(dv[: 2 * rows], w_v[...], (1, 1))
    mine_out[...] = total[:rows]
    other_out[...] = total[rows:]


def assemble_body(width, starts, info, *refs):
    pieces, others, out = refs[:-2], refs[-2], refs[-1]
    at = 0
    for start, ref in zip(starts, pieces):
        columns = ref.shape[1]
        for core, part in ((info[2], ref[...]), (1 - info[2], others[:, at : at + columns])):
            column = pl.multiple_of(start + core * (width // 2), 128)
            out[:, pl.ds(column, columns)] = part
        at += columns


def after(value, *others):
    return lax.optimization_barrier((value, *others))[0]


def partners(count, bit):
    return [(i, i ^ bit) for i in range(count)]


def local(tokens, w_query, w_key, w_value, w_output, out_cotangent):
    clip_count, rows, width = tokens.shape
    assert clip_count == 1
    size = width // H
    half = width // 2
    count = PIECES * rows
    n_seq, n_dp = lax.axis_size("seq"), lax.axis_size("dp")
    pairs = n_seq // PIECES
    seq, place = lax.axis_index("seq"), lax.axis_index("dp")
    info = jnp.stack([seq, place, seq % 2, seq // 2 % 2]).astype(jnp.int32)
    swap = functools.partial(lax.ppermute, axis_name="seq")
    core_links, chip_links = partners(n_seq, 1), partners(n_seq, 2)

    def shift(value, forward):
        total = None
        for d in range(1, pairs):
            links = [(i, i + PIECES * d) for i in range(n_seq - PIECES * d)]
            if not forward:
                links = [(j, i) for i, j in links]
            got = swap(value, perm=links)
            total = got if total is None else total + got
        return total

    tok = tokens.reshape(rows, width)
    cot = out_cotangent.reshape(rows, width)
    tok_f32 = tok.astype(F32)
    tok2 = swap(tok_f32, perm=chip_links)
    tok1 = swap(tok_f32, perm=core_links)
    cot_f32 = after(cot, tok_f32).astype(F32)
    cot2 = swap(cot_f32, perm=chip_links)
    cot1 = swap(cot_f32, perm=core_links)

    columns = lambda i, info: (0, info[2])
    weights = [(w, (width, half), columns) for w in (w_query, w_key, w_value)]
    narrow, wide = (2 * rows, half), (count, half)
    outs = [(narrow, BF16)] * 3 + [((half, size), F32), (narrow, BF16)]
    body = functools.partial(project_body, n_seq, size)
    flops = 2 * 2 * rows * width * half * 3
    q0, k0, v0, state0, rows0 = call(body, info, outs, [tok, tok1, *weights], name="proj0", flops=flops)
    tok2 = after(tok2, state0)
    tok3 = swap(tok2, perm=core_links)
    q1, k1, v1, state, rows1 = call(
        body, info, outs, [tok2, tok3, *weights, state0], name="proj1", flops=flops
    )
    carried = shift(state, True)
    q, k, v, attn, inner = call(
        functools.partial(inside_body, rows, size),
        info,
        [(wide, BF16)] * 3 + [((H // 2, count, count), BF16), (wide, F32)],
        [q0, q1, k0, k1, v0, v1],
        name="inside",
        flops=4 * 4 * count * count * size,
    )
    cot2 = after(cot2, carried)
    cot3 = swap(cot2, perm=core_links)
    cot_all, back = call(
        cotangent_body,
        info,
        [((count, width), BF16), (wide, F32)],
        [cot, cot1, cot2, cot3, (w_output, (half, width), lambda i, info: (info[2], 0))],
        name="cotangent",
        flops=2 * count * width * half,
    )
    carried = after(carried, back, inner)
    mixed, stats = call(
        functools.partial(stats_body, size),
        info,
        [(wide, F32), ((count, 128), F32)],
        [q, carried, inner, back],
        name="stats",
        flops=2 * count * half * size,
    )
    stats_other = swap(stats, perm=core_links)
    factor = 1.0 / math.sqrt(clip_count * n_dp * rows * n_seq)
    chunk_shapes = [
        [((half // 2, columns), F32) for columns in widths] * 2 for widths in WIDTHS
    ]
    scratch = [pltpu.VMEM((half, half), F32)]
    grad_flops = 2 * count * half * half
    normed, d_mixed, own_back, dq, back_scores, *parts_q = call(
        functools.partial(norm_body, rows, size, pairs, n_dp, factor),
        info,
        [
            (wide, F32),
            (wide, BF16),
            ((half // 2, size), F32),
            (wide, BF16),
            ((H // 2, count, count), BF16),
            *chunk_shapes[0],
        ],
        [q, k, v, mixed, back, stats, stats_other, carried, rows0, rows1],
        scratch,
        name="norm",
        flops=2 * count * half * size,
    )
    later = shift(own_back, False)
    normed_other = swap(normed, perm=core_links)

    hops = []
    bit = n_dp // 2
    while bit:
        hops.append(("dp", partners(n_dp, bit)))
        bit //= 2
    bit = n_seq // 2
    while bit >= PIECES:
        hops.append(("seq", partners(n_seq, bit)))
        bit //= 2

    def reduce_all(tensors, fillers):
        owner = [n for n, widths in enumerate(WIDTHS) for _ in widths]
        first = [owner.index(n) for n in range(len(tensors))]
        keeps, sends, made = {}, {}, set()
        steps = [(p + LAG * hop, hop, p) for p in range(len(owner)) for hop in range(len(hops))]
        last, first_hop = None, {}
        for at, (_, hop, p) in enumerate(sorted(steps)):
            for n in range(len(tensors)):
                if n not in made and first[n] <= (p if hop == 0 else 0) + AHEAD:
                    made.add(n)
                    parts = tensors[n](last)
                    for c in range(len(parts) // 2):
                        keeps[first[n] + c] = parts[c]
                        sends[first[n] + c] = parts[len(parts) // 2 + c]
            axis, links = hops[hop]
            if hop == 0 and p - WINDOW in first_hop:
                sends[p] = after(sends[p], first_hop[p - WINDOW])
            if at in fillers:
                last = fillers[at](last)
            got = lax.ppermute(sends[p], axis, links)
            total = (keeps[p] if last is None else after(keeps[p], last)) + got
            last = total
            if hop == 0:
                first_hop[p] = total
            middle = total.shape[0] // 2
            keeps[p], sends[p] = total[:middle], total[middle:]
        chunks = range(len(owner))
        sent = jnp.concatenate([sends[p] for p in chunks], axis=1)
        return [keeps[p] for p in chunks], swap(sent, perm=core_links)

    def weight_grad(grad, name, shapes):
        return call(
            functools.partial(grad_body, pairs, n_dp, factor),
            info,
            shapes,
            [rows0, rows1, grad],
            scratch,
            name=name,
            flops=grad_flops,
        )

    results = {}

    def grad_query(last):
        return parts_q

    def grad_output(last):
        return call(
            functools.partial(grad_out_body, rows, pairs, n_dp, factor),
            info,
            chunk_shapes[1],
            [normed, normed_other, (cot_all, (count, half), columns)],
            scratch,
            name="grad_o",
            flops=grad_flops,
        )

    def grad_key(last):
        dk_inner, dv_inner = call(
            functools.partial(back_rest_body, size),
            info,
            [(wide, F32), (wide, F32)],
            [q, d_mixed, attn, after(back_scores, normed_other)],
            name="back_rest",
            flops=4 * 4 * count * count * size,
        )
        late = after(later, last)
        results["dk"], results["dv"] = call(
            functools.partial(finish_body, size),
            info,
            [(wide, BF16)] * 2,
            [k, v, late, swap(late, perm=chip_links), dk_inner, dv_inner],
            name="finish",
            flops=4 * count * half * size,
        )
        results["key"] = weight_grad(results["dk"], "grad_k", chunk_shapes[2])
        return results["key"]

    def grad_value(last):
        return weight_grad(after(results["dv"], results["key"][0]), "grad_v", chunk_shapes[3])


    def attend(last):
        (results["attended"],) = call(
            functools.partial(attended_body, rows),
            info,
            [((rows, width), BF16)],
            [after(normed, last), normed_other, w_output],
            name="attended",
            flops=2 * rows * width * width,
        )
        return results["attended"]

    def back_tokens(last):
        results["mine"], results["other"] = call(
            functools.partial(tokens_body, rows),
            info,
            [((rows, width), F32)] * 2,
            [after(dq, last), results["dk"], results["dv"], *weights],
            name="d_tokens",
            flops=6 * 2 * rows * width * half,
        )
        return results["mine"]

    own, other_core = reduce_all(
        [grad_query, grad_output, grad_key, grad_value], {4: attend, 7: back_tokens}
    )
    attended, mine, other = results["attended"], results["mine"], results["other"]
    d_tokens = (mine + swap(other, perm=core_links)).astype(BF16)
    starts = []
    for tensor, widths in zip((0, 3, 1, 2), WIDTHS):
        starts += [tensor * width + sum(widths[:c]) for c in range(len(widths))]
    (grads,) = call(
        functools.partial(assemble_body, width, starts),
        info,
        [((width // (n_seq * n_dp), 4 * width), F32)],
        own + [other_core],
        name="assemble",
    )
    return (
        attended.reshape(tokens.shape),
        d_tokens.reshape(tokens.shape),
        grads,
    )


def solution(mesh):
    return jax.shard_map(
        local,
        mesh=mesh,
        in_specs=(
            P(("groups", "dp"), "seq", None),
            P(),
            P(),
            P(),
            P(),
            P(("groups", "dp"), "seq", None),
        ),
        out_specs=(
            P(("groups", "dp"), "seq", None),
            P(("groups", "dp"), "seq", None),
            P(("groups", "seq", "dp"), None),
        ),
        check_vma=False,
    )
```

```python
import functools
import math

import jax
import jax.numpy as jnp
from jax import lax
from jax.experimental import pallas as pl
from jax.experimental.pallas import tpu as pltpu
from jax.sharding import PartitionSpec as P

H = 8
WINDOW, AHEAD = 3, 2
LATE = -1
LAG = 1.5
WIDTHS = ((256, 256), (512,), (512,), (256, 256))
EPSILON = 1e-05
PIECES = 4
F32, BF16 = jnp.float32, jnp.bfloat16
WHOLE = pl.BlockSpec(memory_space=pltpu.VMEM)


def call(body, info, outs, ins, scratch=(), name=None, flops=0):
    arrays, specs, moved = [], [], 0
    for entry in ins:
        if isinstance(entry, tuple):
            array, block, index = entry
            arrays.append(array)
            specs.append(pl.BlockSpec(block, index))
            moved += math.prod(block) * array.dtype.itemsize
        else:
            arrays.append(entry)
            specs.append(WHOLE)
            moved += entry.size * entry.dtype.itemsize
    shapes = [jax.ShapeDtypeStruct(shape, dtype) for shape, dtype in outs]
    moved += sum(math.prod(shape) * jnp.dtype(dtype).itemsize for shape, dtype in outs)
    return pl.pallas_call(
        body,
        name=name,
        out_shape=shapes,
        grid_spec=pltpu.PrefetchScalarGridSpec(
            num_scalar_prefetch=1,
            grid=(1,),
            in_specs=specs,
            out_specs=[WHOLE] * len(shapes),
            scratch_shapes=list(scratch),
        ),
        compiler_params=pltpu.CompilerParams(vmem_limit_bytes=24 * 2**20),
        cost_estimate=pl.CostEstimate(flops=1, bytes_accessed=1, transcendentals=0),
    )(info, *arrays)


def dot(a, b, over=(1, 0)):
    return lax.dot_general(
        a, b, (((over[0],), (over[1],)), ((), ())), preferred_element_type=F32
    )


def head(array, h, size):
    return array[:, h * size : (h + 1) * size]


def causal(info_ref, rows, count):
    seq = info_ref[0]

    def position(dim):
        at = lax.broadcasted_iota(jnp.int32, (count, count), dim)
        piece = jnp.bitwise_xor(at // rows, seq)
        return piece * rows + at % rows

    return position(0) >= position(1)


def across(ref, rows):
    order = [piece ^ 1 for piece in range(PIECES)]
    return jnp.concatenate([ref[piece * rows : (piece + 1) * rows] for piece in order], axis=0)


def project_body(n_seq, size, info, first, second, w_q, w_k, w_v, *rest):
    if len(rest) == 6:
        before, q_out, k_out, v_out, state_out, rows_out = rest
    else:
        before = None
        q_out, k_out, v_out, state_out, rows_out = rest
    width = first.shape[1]
    rows = jnp.concatenate([first[...].astype(BF16), second[...].astype(BF16)], axis=0)
    block = 2 * width // n_seq
    for pair in range(n_seq // PIECES):
        at = pl.ds(pl.multiple_of((pair * 2 + info[3]) * block, block), block)
        for i, ref in enumerate((first, second)):
            count = ref.shape[0]
            rows_out[i * count : (i + 1) * count, pair * block : (pair + 1) * block] = ref[:, at].astype(BF16)
    q_out[...] = dot(rows, w_q[...]).astype(BF16)
    keys = dot(rows, w_k[...]).astype(BF16)
    k_out[...] = keys
    values = dot(rows, w_v[...]).astype(BF16)
    v_out[...] = values
    for h in range(keys.shape[1] // size):
        state = dot(head(keys, h, size), head(values, h, size), (0, 0))
        if before is not None:
            state = state + before[h * size : (h + 1) * size]
        state_out[h * size : (h + 1) * size] = state


def inside_body(rows, size, info, q0, q1, k0, k1, v0, v1, *outs):
    q_out, k_out, v_out, attn_out, mixed_out = outs
    q = jnp.concatenate([q0[...], q1[...]], axis=0)
    k = jnp.concatenate([k0[...], k1[...]], axis=0)
    v = jnp.concatenate([v0[...], v1[...]], axis=0)
    q_out[...], k_out[...], v_out[...] = q, k, v
    mask = causal(info, rows, q.shape[0])
    for h in range(q.shape[1] // size):
        scores = dot(head(q, h, size), head(k, h, size), (1, 1))
        attn = jnp.where(mask, scores, 0.0).astype(BF16)
        attn_out[h] = attn
        mixed_out[:, h * size : (h + 1) * size] = dot(attn, head(v, h, size))


def cotangent_body(info, c0, c1, c2, c3, w_o, cot_out, back_out):
    cot = jnp.concatenate([c[...].astype(BF16) for c in (c0, c1, c2, c3)], axis=0)
    cot_out[...] = cot
    back_out[...] = dot(cot, w_o[...], (1, 1))


def stats_body(size, info, q, carried, inner, back, mixed_out, stats_out):
    for h in range(q.shape[1] // size):
        state = carried[h * size : (h + 1) * size].astype(BF16)
        mixed_out[:, h * size : (h + 1) * size] = inner[:, h * size : (h + 1) * size] + dot(
            head(q, h, size), state
        )
    mixed = mixed_out[...]
    squares = jnp.sum(mixed * mixed, axis=1, keepdims=True)
    cross = jnp.sum(mixed * back[...], axis=1, keepdims=True)
    lane = lax.broadcasted_iota(jnp.int32, stats_out.shape, 1)
    stats_out[...] = jnp.where(lane == 0, squares, cross)


def norm_body(rows, size, pairs, n_dp, factor, info, q, k, v, mixed, back, mine, other, carried, r0, r1, *refs):
    normed_out, d_out, state_out, dq_out, scores_out = refs[:5]
    outs, total = refs[5:-1], refs[-1]
    width = 2 * mixed.shape[1]
    sums = mine[...] + across(other, rows)
    squares, cross = sums[:, 0:1], sums[:, 1:2]
    scale = jnp.sqrt(squares * (1.0 / width) + EPSILON)
    normed = mixed[...] / scale
    normed_out[...] = normed.astype(BF16).astype(F32)
    mean = cross / scale * (1.0 / width)
    d_mixed = ((back[...] - normed * mean) / scale).astype(BF16)
    d_out[...] = d_mixed
    mask = causal(info, rows, q.shape[0])
    heads = q.shape[1] // size
    states = []
    for h in range(heads):
        at = slice(h * size, (h + 1) * size)
        d_head = d_mixed[:, at]
        states.append(dot(q[:, at], d_head, (0, 0)))
        scores = dot(d_head, v[:, at], (1, 1))
        scores = jnp.where(mask, scores, 0.0).astype(BF16)
        scores_out[h] = scores
        state = carried[at].astype(BF16)
        dq_out[:, at] = (dot(scores, k[:, at]) + dot(d_head, state, (1, 1))).astype(BF16)
    for h in range(heads // 2):
        state_out[h * size : (h + 1) * size] = jnp.where(
            info[3] == 0, states[h], states[heads // 2 + h]
        )
    half = r0.shape[0]
    total[...] = (
        dot(r0[...], dq_out[:half], (0, 0)) + dot(r1[...], dq_out[half:], (0, 0))
    ) * factor
    split_rows(info, pairs, n_dp, total, *outs)


def back_rest_body(size, info, q, d_mixed, attn, scores, dk_out, dv_out):
    for h in range(q.shape[1] // size):
        at = slice(h * size, (h + 1) * size)
        dk_out[:, at] = dot(scores[h], q[:, at], (0, 0))
        dv_out[:, at] = dot(attn[h], d_mixed[:, at], (0, 0))


def finish_body(size, info, k, v, later, later_other, dk_in, dv_in, dk_out, dv_out):
    heads = k.shape[1] // size
    for h in range(heads):
        at = slice(h * size, (h + 1) * size)
        half = slice(h % (heads // 2) * size, (h % (heads // 2) + 1) * size)
        is_mine = info[3] == h // (heads // 2)
        state = jnp.where(is_mine, later[half], later_other[half]).astype(BF16)
        dk_out[:, at] = (dk_in[:, at] + dot(v[:, at], state, (1, 1))).astype(BF16)
        dv_out[:, at] = (dv_in[:, at] + dot(k[:, at], state)).astype(BF16)


def split_rows(info, pairs, n_dp, total, *outs):
    keep_outs, send_outs = outs[: len(outs) // 2], outs[len(outs) // 2 :]
    kept = keep_outs[0].shape[0]
    block = total.shape[0] // (pairs * 2 * n_dp)
    seq, place = info[0], info[1]
    for slot in range(pairs * 2 * n_dp):
        i, pair, core = slot // (2 * pairs), slot // 2 % pairs, slot % 2
        owner = jnp.bitwise_xor(seq // PIECES, pair) * 2 + jnp.bitwise_xor(seq % 2, core)
        owner = owner * n_dp + jnp.bitwise_xor(place, i)
        rows = pl.ds(pl.multiple_of(owner * block, block), block)
        at = slot * block
        targets = keep_outs if at < kept else send_outs
        at = at % kept
        start = 0
        for target in targets:
            target[at : at + block] = total[rows, start : start + target.shape[1]]
            start += target.shape[1]


def grad_body(pairs, n_dp, factor, info, r0, r1, grad, *outs):
    outs, total = outs[:-1], outs[-1]
    half = r0.shape[0]
    total[...] = (
        dot(r0[...], grad[:half], (0, 0)) + dot(r1[...], grad[half:], (0, 0))
    ) * factor
    split_rows(info, pairs, n_dp, total, *outs)


def grad_out_body(rows, pairs, n_dp, factor, info, mine, other, cot, *outs):
    outs, total = outs[:-1], outs[-1]
    core, chip = info[2], info[3]
    block = 2 * mine.shape[1] // (2 * pairs)
    per_core = mine.shape[1] // block
    order = [piece ^ 1 for piece in range(PIECES)]
    for pair in range(pairs):
        index = pair * 2 + chip
        at = pl.ds(pl.multiple_of(index % per_core * block, block), block)
        is_mine = index // per_core == core
        parts = [
            jnp.where(is_mine, mine[p * rows : (p + 1) * rows, at], other[order[p] * rows : (order[p] + 1) * rows, at])
            for p in range(PIECES)
        ]
        left = jnp.concatenate(parts, axis=0).astype(BF16)
        total[pair * block : (pair + 1) * block] = dot(left, cot[...], (0, 0)) * factor
    split_rows(info, pairs, n_dp, total, *outs)


def attended_body(rows, info, mine, other, w_o, out):
    half = mine.shape[1]
    core = info[2]
    total = None
    for array, at in ((mine[:rows], core), (other[rows : 2 * rows], 1 - core)):
        weight = w_o[pl.ds(pl.multiple_of(at * half, half), half), :]
        part = dot(array.astype(BF16), weight)
        total = part if total is None else total + part
    out[...] = total.astype(BF16)


def tokens_body(rows, info, dq, dk, dv, w_q, w_k, w_v, mine_out, other_out):
    total = dot(dq[: 2 * rows], w_q[...], (1, 1))
    total = total + dot(dk[: 2 * rows], w_k[...], (1, 1))
    total = total + dot(dv[: 2 * rows], w_v[...], (1, 1))
    mine_out[...] = total[:rows]
    other_out[...] = total[rows:]


def assemble_body(width, starts, info, *refs):
    pieces, (early, late), out = refs[:-3], refs[-3:-1], refs[-1]
    at = 0
    for n, (start, ref) in enumerate(zip(starts, pieces)):
        columns = ref.shape[1]
        others = early if n < len(pieces) + LATE else late
        if n == len(pieces) + LATE:
            at = 0
        for core, part in ((info[2], ref[...]), (1 - info[2], others[:, at : at + columns])):
            column = pl.multiple_of(start + core * (width // 2), 128)
            out[:, pl.ds(column, columns)] = part
        at += columns


def after(value, *others):
    return lax.optimization_barrier((value, *others))[0]


def partners(count, bit):
    return [(i, i ^ bit) for i in range(count)]


def local(tokens, w_query, w_key, w_value, w_output, out_cotangent):
    clip_count, rows, width = tokens.shape
    assert clip_count == 1
    size = width // H
    half = width // 2
    count = PIECES * rows
    n_seq, n_dp = lax.axis_size("seq"), lax.axis_size("dp")
    pairs = n_seq // PIECES
    seq, place = lax.axis_index("seq"), lax.axis_index("dp")
    info = jnp.stack([seq, place, seq % 2, seq // 2 % 2]).astype(jnp.int32)
    swap = functools.partial(lax.ppermute, axis_name="seq")
    core_links, chip_links = partners(n_seq, 1), partners(n_seq, 2)

    def shift(value, forward):
        total = None
        for d in range(1, pairs):
            links = [(i, i + PIECES * d) for i in range(n_seq - PIECES * d)]
            if not forward:
                links = [(j, i) for i, j in links]
            got = swap(value, perm=links)
            total = got if total is None else total + got
        return total

    tok = tokens.reshape(rows, width)
    cot = out_cotangent.reshape(rows, width)
    tok_f32 = tok.astype(F32)
    tok2 = swap(tok_f32, perm=chip_links)
    tok1 = swap(tok_f32, perm=core_links)
    cot_f32 = after(cot, tok_f32).astype(F32)
    cot2 = swap(cot_f32, perm=chip_links)
    cot1 = swap(cot_f32, perm=core_links)

    columns = lambda i, info: (0, info[2])
    weights = [(w, (width, half), columns) for w in (w_query, w_key, w_value)]
    narrow, wide = (2 * rows, half), (count, half)
    outs = [(narrow, BF16)] * 3 + [((half, size), F32), (narrow, BF16)]
    body = functools.partial(project_body, n_seq, size)
    flops = 2 * 2 * rows * width * half * 3
    q0, k0, v0, state0, rows0 = call(body, info, outs, [tok, tok1, *weights], name="proj0", flops=flops)
    tok2 = after(tok2, state0)
    tok3 = swap(tok2, perm=core_links)
    q1, k1, v1, state, rows1 = call(
        body, info, outs, [tok2, tok3, *weights, state0], name="proj1", flops=flops
    )
    carried = shift(state, True)
    q, k, v, attn, inner = call(
        functools.partial(inside_body, rows, size),
        info,
        [(wide, BF16)] * 3 + [((H // 2, count, count), BF16), (wide, F32)],
        [q0, q1, k0, k1, v0, v1],
        name="inside",
        flops=4 * 4 * count * count * size,
    )
    cot2 = after(cot2, carried)
    cot3 = swap(cot2, perm=core_links)
    cot_all, back = call(
        cotangent_body,
        info,
        [((count, width), BF16), (wide, F32)],
        [cot, cot1, cot2, cot3, (w_output, (half, width), lambda i, info: (info[2], 0))],
        name="cotangent",
        flops=2 * count * width * half,
    )
    carried = after(carried, back, inner)
    mixed, stats = call(
        functools.partial(stats_body, size),
        info,
        [(wide, F32), ((count, 128), F32)],
        [q, carried, inner, back],
        name="stats",
        flops=2 * count * half * size,
    )
    stats_other = swap(stats, perm=core_links)
    factor = 1.0 / math.sqrt(clip_count * n_dp * rows * n_seq)
    chunk_shapes = [
        [((half // 2, columns), F32) for columns in widths] * 2 for widths in WIDTHS
    ]
    scratch = [pltpu.VMEM((half, half), F32)]
    grad_flops = 2 * count * half * half
    normed, d_mixed, own_back, dq, back_scores, *parts_q = call(
        functools.partial(norm_body, rows, size, pairs, n_dp, factor),
        info,
        [
            (wide, F32),
            (wide, BF16),
            ((half // 2, size), F32),
            (wide, BF16),
            ((H // 2, count, count), BF16),
            *chunk_shapes[0],
        ],
        [q, k, v, mixed, back, stats, stats_other, carried, rows0, rows1],
        scratch,
        name="norm",
        flops=2 * count * half * size,
    )
    later = shift(own_back, False)
    normed_other = swap(normed, perm=core_links)

    hops = []
    bit = n_dp // 2
    while bit:
        hops.append(("dp", partners(n_dp, bit)))
        bit //= 2
    bit = n_seq // 2
    while bit >= PIECES:
        hops.append(("seq", partners(n_seq, bit)))
        bit //= 2

    def reduce_all(tensors, fillers):
        owner = [n for n, widths in enumerate(WIDTHS) for _ in widths]
        first = [owner.index(n) for n in range(len(tensors))]
        keeps, sends, made = {}, {}, set()
        steps = [(p + LAG * hop, hop, p) for p in range(len(owner)) for hop in range(len(hops))]
        last, first_hop = None, {}
        for at, (_, hop, p) in enumerate(sorted(steps)):
            for n in range(len(tensors)):
                if n not in made and first[n] <= (p if hop == 0 else 0) + AHEAD:
                    made.add(n)
                    parts = tensors[n](last)
                    for c in range(len(parts) // 2):
                        keeps[first[n] + c] = parts[c]
                        sends[first[n] + c] = parts[len(parts) // 2 + c]
            axis, links = hops[hop]
            if hop == 0 and p - WINDOW in first_hop:
                sends[p] = after(sends[p], first_hop[p - WINDOW])
            if at in fillers:
                last = fillers[at](last)
            got = lax.ppermute(sends[p], axis, links)
            total = (keeps[p] if last is None else after(keeps[p], last)) + got
            last = total
            if hop == 0:
                first_hop[p] = total
            middle = total.shape[0] // 2
            keeps[p], sends[p] = total[:middle], total[middle:]
        chunks = range(len(owner))
        sent = [
            swap(jnp.concatenate([sends[p] for p in group], axis=1), perm=core_links)
            for group in (chunks[:LATE], chunks[LATE:])
        ]
        return [keeps[p] for p in chunks], sent

    def weight_grad(grad, name, shapes):
        return call(
            functools.partial(grad_body, pairs, n_dp, factor),
            info,
            shapes,
            [rows0, rows1, grad],
            scratch,
            name=name,
            flops=grad_flops,
        )

    results = {}

    def grad_query(last):
        return parts_q

    def grad_output(last):
        return call(
            functools.partial(grad_out_body, rows, pairs, n_dp, factor),
            info,
            chunk_shapes[1],
            [normed, normed_other, (cot_all, (count, half), columns)],
            scratch,
            name="grad_o",
            flops=grad_flops,
        )

    def grad_key(last):
        dk_inner, dv_inner = call(
            functools.partial(back_rest_body, size),
            info,
            [(wide, F32), (wide, F32)],
            [q, d_mixed, attn, after(back_scores, normed_other)],
            name="back_rest",
            flops=4 * 4 * count * count * size,
        )
        late = after(later, last)
        results["dk"], results["dv"] = call(
            functools.partial(finish_body, size),
            info,
            [(wide, BF16)] * 2,
            [k, v, late, swap(late, perm=chip_links), dk_inner, dv_inner],
            name="finish",
            flops=4 * count * half * size,
        )
        results["key"] = weight_grad(results["dk"], "grad_k", chunk_shapes[2])
        return results["key"]

    def grad_value(last):
        return weight_grad(after(results["dv"], results["key"][0]), "grad_v", chunk_shapes[3])


    def attend(last):
        (results["attended"],) = call(
            functools.partial(attended_body, rows),
            info,
            [((rows, width), BF16)],
            [after(normed, last), normed_other, w_output],
            name="attended",
            flops=2 * rows * width * width,
        )
        return results["attended"]

    def back_tokens(last):
        results["mine"], results["other"] = call(
            functools.partial(tokens_body, rows),
            info,
            [((rows, width), F32)] * 2,
            [after(dq, last), results["dk"], results["dv"], *weights],
            name="d_tokens",
            flops=6 * 2 * rows * width * half,
        )
        return results["mine"]

    own, other_core = reduce_all(
        [grad_query, grad_output, grad_key, grad_value], {3: attend, 6: back_tokens}
    )
    attended, mine, other = results["attended"], results["mine"], results["other"]
    d_tokens = (mine + swap(other, perm=core_links)).astype(BF16)
    starts = []
    for tensor, widths in zip((0, 3, 1, 2), WIDTHS):
        starts += [tensor * width + sum(widths[:c]) for c in range(len(widths))]
    (grads,) = call(
        functools.partial(assemble_body, width, starts),
        info,
        [((width // (n_seq * n_dp), 4 * width), F32)],
        own + other_core,
        name="assemble",
    )
    return (
        attended.reshape(tokens.shape),
        d_tokens.reshape(tokens.shape),
        grads,
    )


def solution(mesh):
    return jax.shard_map(
        local,
        mesh=mesh,
        in_specs=(
            P(("groups", "dp"), "seq", None),
            P(),
            P(),
            P(),
            P(),
            P(("groups", "dp"), "seq", None),
        ),
        out_specs=(
            P(("groups", "dp"), "seq", None),
            P(("groups", "dp"), "seq", None),
            P(("groups", "seq", "dp"), None),
        ),
        check_vma=False,
    )
```
